256 devices in a mesh: row: 16 (over z, x_lo), col: 16 (over y, x_hi, core).
Axes of the slice: x: 4 (x_hi: 2, x_lo: 2; x = x_hi * 2 + x_lo), y: 4, z: 8, core: 2. Of those that a mesh axis runs over, the one named last changes fastest.
Arguments:
- corner: bfloat16 [16, 16, 64, 64], P('row', 'col'), may hold values from -0.75 to 0.75
- top_edge: bfloat16 [16, 16, 64, 1024], P('row', 'col'), may hold values from -0.75 to 0.75
- left_edge: bfloat16 [16, 16, 64, 1024], P('row', 'col'), may hold values from -0.75 to 0.75
- site_tensor: bfloat16 [16, 16, 2, 4, 4, 4, 4], P('row', 'col'), may hold values from -1.3984375 to 1.3984375
- sketch: bfloat16 [16, 16, 64, 1024], P('row', 'col'), may hold values from -0.1875 to 0.1875
- grad_left: bfloat16 [16, 16, 64, 1024], P('row', 'col'), may hold values from -0.019897461 to 0.019897461
- grad_top: bfloat16 [16, 16, 64, 1024], P('row', 'col'), may hold values from -0.019897461 to 0.019897461
Outputs:
- corner_grad: bfloat16 [16, 16, 64, 64], P('row', 'col')
- top_grad: bfloat16 [16, 16, 64, 1024], P('row', 'col')
- left_grad: bfloat16 [16, 16, 64, 1024], P('row', 'col')
- site_grad: float32 [16, 16, 2, 4, 4, 4, 4], P('row', 'col')
The draws below stay inside these ranges and needn't reach their ends.
All inputs are finite; a program needn't handle non-finite values.
Results may differ from the reference program's by a relative error of at most 0.014.
Values may be sent and summed in bfloat16 or wider, within the bound.
No kernel may reach another device: no remote copies, remote signals or barrier semaphores. Data moves between devices by JAX's collectives and lax.ppermute only.
A program may use at most 64 MiB of HBM per device.

```python
import jax
import jax.numpy as jnp
from jax import lax

CHI = 64
D = 4
PHYS = 2
DD = 16
NR = 16
NC = 16
N_ROW = 16
N_COL = 16


def levels(own_key, shape, pieces, low, top_value):
    def one(axis_at, shards_of):
        steps = jax.random.uniform(jax.random.fold_in(jax.random.fold_in(own_key, 6), axis_at), (shards_of,), jnp.float32, low / len(pieces), top_value / len(pieces))
        return jnp.repeat(jnp.exp(steps), shape[axis_at] // shards_of).reshape((-1,) + (1,) * (len(shape) - axis_at - 1))

    gain = one(*pieces[0])
    for cut in pieces[1:]:
        gain = gain * one(*cut)
    return gain


def normal_values(rng, dims, scale, reach, cuts=(), kind=jnp.bfloat16):
    entries = scale * jax.random.normal(rng, dims, jnp.float32)
    if cuts:
        entries = entries * levels(rng, dims, cuts, -0.22, 0.18)
    return jnp.clip(entries, -reach, reach).astype(kind)


def setup_inputs(seed: int = 0) -> dict:
    key_of = jax.random.split(jax.random.key(seed), 8)
    corner = normal_values(key_of[0], (NR, NC, CHI, CHI), CHI ** -0.5, 0.75, ((0, 16), (1, 16)))
    top_edge = normal_values(key_of[1], (NR, NC, CHI, DD * CHI), CHI ** -0.5, 0.75, ((0, 16), (1, 16)))
    left_edge = normal_values(key_of[2], (NR, NC, CHI, DD * CHI), CHI ** -0.5, 0.75, ((0, 16), (1, 16)))
    site_tensor = normal_values(key_of[3], (NR, NC, PHYS, D, D, D, D), 0.22, 1.3984375, ((0, 16), (1, 16)))
    sketch = normal_values(key_of[4], (NR, NC, CHI, DD * CHI), (DD * CHI) ** -0.5, 0.1875, ((0, 16), (1, 16)))
    grad_left = normal_values(key_of[5], (NR, NC, CHI, DD * CHI), 0.003, 0.019897461, ((0, 16), (1, 16)))
    grad_top = normal_values(key_of[6], (NR, NC, CHI, DD * CHI), 0.003, 0.019897461, ((0, 16), (1, 16)))
    return dict(corner=corner, top_edge=top_edge, left_edge=left_edge, site_tensor=site_tensor, sketch=sketch, grad_left=grad_left, grad_top=grad_top)


def contract(form, left_op, right_op):
    return jnp.einsum(form, left_op.astype(jnp.float32), right_op.astype(jnp.float32))


def mat_prod(left_op, right_op):
    return jnp.dot(left_op, right_op, preferred_element_type=jnp.float32)


def layers(corner_used, top_used, left_used, tensor_site):
    env_dim = corner_used.shape[0]
    bond_dim = tensor_site.shape[1]
    leg_dim = bond_dim * bond_dim
    top_mat = top_used
    first_prod = mat_prod(corner_used, top_mat).astype(jnp.bfloat16)
    left_three = left_used.reshape(env_dim, leg_dim, env_dim)
    second_prod = contract('lwm,lx->wmx', left_three, first_prod).astype(jnp.bfloat16)
    second_six = second_prod.reshape(bond_dim, bond_dim, env_dim, bond_dim, bond_dim, env_dim)
    ket_layer = contract('abmcet,pcavs->pbmevst', second_six, tensor_site).astype(jnp.bfloat16)
    return top_mat, first_prod, second_six, ket_layer


def forward_site(operands):
    corner_used, top_used, left_used, tensor_site, own_sketch, own_gleft, own_gtop = operands
    top_mat, first_prod, second_six, ket_layer = layers(corner_used, top_used, left_used, tensor_site)
    order_total = own_sketch.shape[1]
    quadrant = contract('pbmevst,pebxz->szmvxt', ket_layer, tensor_site).astype(jnp.bfloat16)
    quadrant = quadrant.reshape(order_total, order_total)
    sketched = mat_prod(own_sketch, quadrant.T).astype(jnp.bfloat16)
    downward = mat_prod(own_gleft, quadrant).astype(jnp.bfloat16)
    rightward = mat_prod(own_gtop, quadrant.T).astype(jnp.bfloat16)
    return sketched, downward, rightward


def backward_site(operands):
    corner_used, top_used, left_used, tensor_site, left_factor, right_factor = operands
    top_mat, first_prod, second_six, ket_layer = layers(corner_used, top_used, left_used, tensor_site)
    env_dim = corner_used.shape[0]
    bond_dim = tensor_site.shape[1]
    leg_dim = bond_dim * bond_dim
    grad_quad = jnp.dot(left_factor.T, right_factor, preferred_element_type=jnp.float32).astype(jnp.bfloat16)
    grad_quad = grad_quad.reshape(bond_dim, bond_dim, env_dim, bond_dim, bond_dim, env_dim)
    grad_ket = contract('szmvxt,pebxz->pbmevst', grad_quad, tensor_site).astype(jnp.bfloat16)
    bra_part = contract('pbmevst,szmvxt->pebxz', ket_layer, grad_quad)
    grad_second = contract('pbmevst,pcavs->abmcet', grad_ket, tensor_site).astype(jnp.bfloat16)
    ket_part = contract('abmcet,pbmevst->pcavs', second_six, grad_ket)
    grad_mat = grad_second.reshape(leg_dim, env_dim, leg_dim * env_dim)
    left_three = left_used.reshape(env_dim, leg_dim, env_dim)
    grad_first = contract('lwm,wmx->lx', left_three, grad_mat).astype(jnp.bfloat16)
    grad_lefted = contract('lx,wmx->lwm', first_prod, grad_mat).astype(jnp.bfloat16).reshape(left_used.shape)
    grad_topped = mat_prod(corner_used.T, grad_first).astype(jnp.bfloat16)
    grad_cornered = mat_prod(grad_first, top_mat.T).astype(jnp.bfloat16)
    return grad_cornered, grad_topped, grad_lefted, ket_part + bra_part


def flatten(tensor):
    return tensor.reshape((N_ROW * N_COL,) + tensor.shape[2:])


def unflatten(tensor):
    return tensor.reshape((N_ROW, N_COL) + tensor.shape[1:])


def reference(corner, top_edge, left_edge, site_tensor, sketch, grad_left, grad_top):
    corner_used = jnp.roll(corner, (1, 1), axis=(0, 1))
    top_used = jnp.roll(top_edge, 1, axis=0)
    left_used = jnp.roll(left_edge, 1, axis=1)
    used = (flatten(corner_used), flatten(top_used), flatten(left_used), flatten(site_tensor))
    sketched, downward, rightward = lax.map(forward_site, used + (flatten(sketch), flatten(grad_left), flatten(grad_top)))
    sketched = unflatten(sketched)
    downward = unflatten(downward)
    rightward = unflatten(rightward)
    sketch_below = jnp.roll(sketched, -1, axis=0)
    sketch_beside = jnp.roll(sketched, -1, axis=1)
    arrived = (jnp.roll(downward, 1, axis=0).astype(jnp.float32) + jnp.roll(rightward, 1, axis=1).astype(jnp.float32)).astype(jnp.bfloat16)
    left_factor = jnp.concatenate([grad_left, sketch_beside, arrived], axis=2)
    right_factor = jnp.concatenate([sketch_below, grad_top, sketch], axis=2)
    grad_cornered, grad_topped, grad_lefted, site_grad = lax.map(backward_site, used + (flatten(left_factor), flatten(right_factor)))
    corner_grad = jnp.roll(unflatten(grad_cornered), (-1, -1), axis=(0, 1))
    top_grad = jnp.roll(unflatten(grad_topped), -1, axis=0)
    left_grad = jnp.roll(unflatten(grad_lefted), -1, axis=1)
    return corner_grad, top_grad, left_grad, unflatten(site_grad)
```

```python
import functools

import jax
import jax.numpy as jnp
from jax import lax
from jax.experimental import pallas as pl
from jax.experimental.pallas import tpu as pltpu
from jax.sharding import PartitionSpec as P

BF = jnp.bfloat16
F32 = jnp.float32
CHI = 64
DD = 16
ORDER = DD * CHI
HALF = CHI // 2
WIDE = 2 * CHI


def dot(lhs, rhs):
    return jnp.dot(lhs, rhs, preferred_element_type=F32)


def dot_nt(lhs, rhs):
    return lax.dot_general(lhs, rhs, (((1,), (1,)), ((), ())), preferred_element_type=F32)


def dot_tn(lhs, rhs):
    return lax.dot_general(lhs, rhs, (((0,), (0,)), ((), ())), preferred_element_type=F32)


def iota(shape, axis):
    return lax.broadcasted_iota(jnp.int32, shape, axis)


def first_half(shape):
    return iota(shape, 1) % WIDE < CHI


def to_rows(nat, rows_ref, out_ref, column):
    value = nat.astype(F32)
    rows_ref[...] = jnp.concatenate([value, value], axis=0).T
    low = first_half((DD, WIDE))
    for at in range(HALF):
        even = rows_ref[pl.ds(2 * at, DD, stride=CHI), :]
        odd = rows_ref[pl.ds(2 * at + 1, DD, stride=CHI), :]
        out_ref[at * DD : (at + 1) * DD, column : column + WIDE] = jnp.where(low, even, odd).astype(BF)


def from_rows(value, rows_ref):
    for at in range(HALF):
        tile = value[at * DD : (at + 1) * DD, :]
        rows_ref[pl.ds(2 * at, DD, stride=CHI), :] = tile
        rows_ref[pl.ds(2 * at + 1, DD, stride=CHI), :] = tile
    turned = rows_ref[...].T
    even = iota((CHI, ORDER), 1) % 2 == 0
    return jnp.where(even, turned[:CHI], turned[CHI:])


def spread(nat, out_ref, row):
    value = nat.astype(F32)
    low = first_half((CHI, WIDE))
    zero = jnp.zeros((CHI, WIDE), F32)
    for pair in range(DD // 2):
        tile = value[:, pair * WIDE : (pair + 1) * WIDE]
        swapped = pltpu.roll(tile, CHI, 1)
        at = 2 * pair * WIDE
        out_ref[row : row + CHI, at : at + WIDE] = jnp.where(low, tile, zero).astype(BF)
        out_ref[row + CHI : row + WIDE, at : at + WIDE] = jnp.where(low, zero, swapped).astype(BF)
        at = at + WIDE
        out_ref[row : row + CHI, at : at + WIDE] = jnp.where(low, swapped, zero).astype(BF)
        out_ref[row + CHI : row + WIDE, at : at + WIDE] = jnp.where(low, zero, tile).astype(BF)


def gather_pair(value):
    low = first_half((CHI, WIDE))
    even, odd = value[:CHI], value[CHI:]
    stay = jnp.where(low, even[:, :WIDE], odd[:, WIDE:])
    move = jnp.where(low, even[:, WIDE:], odd[:, :WIDE])
    return stay + pltpu.roll(move, CHI, 1)


def leg_maps():
    column = iota((DD, 2 * WIDE), 1)
    small = iota((DD, 2 * WIDE), 0)
    ket_c = ((column // 4) % 4) * 4 + column // 64 == small
    bra_c = (column % 4) * 4 + (column // 16) % 4 == small
    return ket_c.astype(BF), bra_c.astype(BF)


def prepare_kernel(site_ref, sketch_ref, gtop_ref, gleft_ref, a_ref, ket_ref, bra_ref, cols_ref, turned_ref, gwide_ref, rows_ref):
    ket_map, bra_map = leg_maps()
    total = None
    for phys in range(2):
        site = site_ref[phys]
        ket = dot_tn(ket_map, dot_tn(site, ket_map).astype(BF))
        bra = dot_tn(bra_map, dot_tn(site, bra_map).astype(BF))
        ket_ref[phys] = ket.astype(BF)
        bra_ref[phys] = bra.astype(BF)
        total = ket * bra if total is None else total + ket * bra
    a_ref[...] = total.astype(BF)
    to_rows(gtop_ref[...], rows_ref, cols_ref, 0)
    to_rows(sketch_ref[...], rows_ref, cols_ref, WIDE)
    turned_ref[...] = cols_ref[...].T
    spread(gleft_ref[...], gwide_ref, 0)


def forward_kernel(
    corner_ref, top_ref, left_ref, a_ref, turned_ref, gwide_ref,
    sketched_ref, downward_ref, rightward_ref, tops_ref, first_ref, lwide_ref, second_ref, rows_ref, quad_ref,
):
    to_rows(top_ref[...], rows_ref, tops_ref, 0)
    corner = corner_ref[...]
    nothing = jnp.zeros((CHI, CHI), BF)
    corner_two = jnp.concatenate(
        [jnp.concatenate([corner, nothing], axis=1), jnp.concatenate([nothing, corner], axis=1)], axis=0
    )
    first_ref[...] = dot_nt(tops_ref[...], corner_two).astype(BF)
    spread(left_ref[...], lwide_ref, 0)

    def second_step(pair, carry):
        at = pl.multiple_of(pair * 2 * WIDE, 2 * WIDE)
        block = dot(first_ref[...], lwide_ref[:, pl.ds(at, 2 * WIDE)]).astype(BF)
        row = pl.multiple_of(pair * 2 * DD, 2 * DD)
        for one in range(HALF):
            piece = block[one * DD : (one + 1) * DD]
            second_ref[pl.ds(row, DD), one * WIDE : (one + 1) * WIDE] = piece[:, :WIDE]
            second_ref[pl.ds(row + DD, DD), one * WIDE : (one + 1) * WIDE] = piece[:, WIDE:]
        return carry

    lax.fori_loop(0, DD // 2, second_step, 0, unroll=2)

    def quad_step(pair, carry):
        at = pl.multiple_of(pair * 2 * WIDE, 2 * WIDE)
        block = dot(a_ref[...], second_ref[:, pl.ds(at, 2 * WIDE)]).astype(BF)
        row = pl.multiple_of(pair * 2 * DD, 2 * DD)
        for leg in range(DD):
            piece = block[leg * DD : (leg + 1) * DD]
            quad_ref[pl.ds(row, DD), leg * WIDE : (leg + 1) * WIDE] = piece[:, :WIDE]
            quad_ref[pl.ds(row + DD, DD), leg * WIDE : (leg + 1) * WIDE] = piece[:, WIDE:]
        return carry

    lax.fori_loop(0, HALF // 2, quad_step, 0, unroll=4)

    for pair in range(DD // 2):
        at = pair * 2 * WIDE
        block = dot(turned_ref[...], quad_ref[:, at : at + 2 * WIDE])
        rightward_ref[:, pair * WIDE : (pair + 1) * WIDE] = gather_pair(block[:WIDE]).astype(BF)
        sketched_ref[:, pair * WIDE : (pair + 1) * WIDE] = gather_pair(block[WIDE:]).astype(BF)
    down = dot_nt(quad_ref[...], gwide_ref[...])
    downward_ref[...] = from_rows(down, rows_ref).astype(BF)


def backward_kernel(
    below_ref, beside_ref, above_ref, behind_ref, cols_ref, gwide_ref, a_ref, tops_ref, first_ref, lwide_ref, corner_ref,
    top_out_ref, corner_out_ref, left_out_ref, dquad_ref, rows_ref, right_ref, left_ref, dsecond_ref,
):
    to_rows(below_ref[...], rows_ref, right_ref, 0)
    right_ref[:, WIDE:] = cols_ref[...]
    left_ref[:WIDE, :] = gwide_ref[...]
    spread(beside_ref[...], left_ref, WIDE)
    arrived = (above_ref[...].astype(F32) + behind_ref[...].astype(F32)).astype(BF)
    spread(arrived, left_ref, 2 * WIDE)

    def dquad_step(pair, carry):
        at = pl.multiple_of(pair * 2 * WIDE, 2 * WIDE)
        block = dot(right_ref[...], left_ref[:, pl.ds(at, 2 * WIDE)]).astype(BF)
        row = pl.multiple_of(pair * 2 * DD, 2 * DD)
        for one in range(HALF):
            piece = block[one * DD : (one + 1) * DD]
            dquad_ref[pl.ds(row, DD), one * WIDE : (one + 1) * WIDE] = piece[:, :WIDE]
            dquad_ref[pl.ds(row + DD, DD), one * WIDE : (one + 1) * WIDE] = piece[:, WIDE:]
        return carry

    lax.fori_loop(0, DD // 2, dquad_step, 0, unroll=2)
    a_turned = a_ref[...].T

    def dsecond_step(pair, carry):
        at = pl.multiple_of(pair * 2 * WIDE, 2 * WIDE)
        block = dot(a_turned, dquad_ref[:, pl.ds(at, 2 * WIDE)]).astype(BF)
        row = pl.multiple_of(pair * 2 * DD, 2 * DD)
        for leg in range(DD):
            piece = block[leg * DD : (leg + 1) * DD]
            dsecond_ref[pl.ds(row, DD), leg * WIDE : (leg + 1) * WIDE] = piece[:, :WIDE]
            dsecond_ref[pl.ds(row + DD, DD), leg * WIDE : (leg + 1) * WIDE] = piece[:, WIDE:]
        return carry

    lax.fori_loop(0, HALF // 2, dsecond_step, 0, unroll=4)

    first_turned = first_ref[...].T
    for pair in range(DD // 2):
        at = pair * 2 * WIDE
        block = dot(first_turned, dsecond_ref[:, at : at + 2 * WIDE])
        left_out_ref[:, pair * WIDE : (pair + 1) * WIDE] = gather_pair(block).astype(BF)
    dfirst = dot_nt(dsecond_ref[...], lwide_ref[...]).astype(BF)
    corner = corner_ref[...]
    nothing = jnp.zeros((CHI, CHI), BF)
    corner_two = jnp.concatenate(
        [jnp.concatenate([corner, nothing], axis=1), jnp.concatenate([nothing, corner], axis=1)], axis=0
    )
    dtop = dot(dfirst, corner_two)
    top_out_ref[...] = from_rows(dtop, rows_ref).astype(BF)
    dcorner = dot_tn(dfirst, tops_ref[...])
    corner_out_ref[...] = (dcorner[:CHI, :CHI] + pltpu.roll(dcorner[CHI:], CHI, 1)[:, :CHI]).astype(BF)


def split(value):
    high = value.astype(BF)
    return high, (value - high.astype(F32)).astype(BF)


def site_kernel(dquad_ref, second_ref, ket_ref, bra_ref, out_ref):
    grad = dot_nt(dquad_ref[...], second_ref[...])
    ket_map, bra_map = leg_maps()
    for phys in range(2):
        total = None
        for other_ref, leg_map in ((ket_ref, bra_map), (bra_ref, ket_map)):
            for part in split(grad * other_ref[phys].astype(F32)):
                half = dot_nt(leg_map, part)
                for piece in split(half):
                    term = dot_nt(piece, leg_map)
                    total = term if total is None else total + term
        out_ref[phys] = total


def shape(*dims, dtype=BF):
    return jax.ShapeDtypeStruct(dims, dtype)


def call(kernel, outs, scratch, flops, moved):
    return pl.pallas_call(
        kernel,
        out_shape=outs,
        scratch_shapes=scratch,
        compiler_params=pltpu.CompilerParams(vmem_limit_bytes=24 << 20),
        cost_estimate=pl.CostEstimate(flops=flops, bytes_accessed=moved, transcendentals=0),
    )


def from_behind(value, axis, by):
    length = lax.axis_size(axis)
    return lax.ppermute(value, axis, [(i, (i + by) % length) for i in range(length)])


def local(corner, top_edge, left_edge, site_tensor, sketch, grad_left, grad_top):
    own_corner = corner[0, 0]
    own_top = top_edge[0, 0]
    own_left = left_edge[0, 0]
    own_sketch = sketch[0, 0]
    own_gleft = grad_left[0, 0]
    own_gtop = grad_top[0, 0]
    site = site_tensor.reshape(2, DD, DD)
    corner_above, top_used = from_behind((own_corner, own_top), "row", 1)
    corner_used, left_used = from_behind((corner_above, own_left), "col", 1)
    rows = pltpu.VMEM((ORDER, WIDE), F32)
    a_mat, ket, bra, cols, turned, gwide = call(
        prepare_kernel,
        (
            shape(256, 256), shape(2, 256, 256), shape(2, 256, 256), shape(512, 256), shape(256, 512), shape(128, 2048),
        ),
        [rows],
        10**7, 2 * 10**6,
    )(site, own_sketch, own_gtop, own_gleft)
    sketched, downward, rightward, tops, first, lwide, second = call(
        forward_kernel,
        (
            shape(CHI, ORDER), shape(CHI, ORDER), shape(CHI, ORDER),
            shape(512, WIDE), shape(512, WIDE), shape(WIDE, 2048), shape(256, 4096),
        ),
        [rows, pltpu.VMEM((512, 2048), BF)],
        2 * 10**9, 4 * 10**6,
    )(corner_used, top_used, left_used, a_mat, turned, gwide)
    sketch_below = from_behind(sketched, "row", -1)
    sketch_beside = from_behind(sketched, "col", -1)
    from_above = from_behind(downward, "row", 1)
    from_left = from_behind(rightward, "col", 1)
    grad_topped, grad_cornered, grad_lefted, dquad = call(
        backward_kernel,
        (shape(CHI, ORDER), shape(CHI, CHI), shape(CHI, ORDER), shape(256, 4096)),
        [rows, pltpu.VMEM((512, 384), BF), pltpu.VMEM((384, 2048), BF), pltpu.VMEM((512, 2048), BF)],
        3 * 10**9, 6 * 10**6,
    )(sketch_below, sketch_beside, from_above, from_left, cols, gwide, a_mat, tops, first, lwide, corner_used)
    top_result, corner_mid = from_behind((grad_topped, grad_cornered), "row", -1)
    left_result, corner_result = from_behind((grad_lefted, corner_mid), "col", -1)
    site_result = call(
        site_kernel, shape(2, DD, DD, dtype=F32), [], 10**9, 5 * 10**6
    )(dquad, second, ket, bra)
    return (
        corner_result[None, None],
        top_result[None, None],
        left_result[None, None],
        site_result.reshape(site_tensor.shape),
    )


def solution(mesh):
    flat = P("row", "col", None, None)
    deep = P("row", "col", None, None, None, None, None)
    return jax.shard_map(
        local,
        mesh=mesh,
        in_specs=(flat, flat, flat, deep, flat, flat, flat),
        out_specs=(flat, flat, flat, deep),
        check_vma=False,
    )
```

```python
import jax
import jax.numpy as jnp
from jax import lax
from jax.experimental import pallas as pl
from jax.experimental.pallas import tpu as pltpu
from jax.sharding import PartitionSpec as P


BF = jnp.bfloat16
F32 = jnp.float32
CHI = 64
DD = 16
ORDER = DD * CHI
HALF = CHI // 2
WIDE = 2 * CHI
PREP = 20 << 20


def dot(lhs, rhs):
    return jnp.dot(lhs, rhs, preferred_element_type=F32)


def dot_nt(lhs, rhs):
    return lax.dot_general(lhs, rhs, (((1,), (1,)), ((), ())), preferred_element_type=F32)


def dot_tn(lhs, rhs):
    return lax.dot_general(lhs, rhs, (((0,), (0,)), ((), ())), preferred_element_type=F32)


def iota(shape, axis):
    return lax.broadcasted_iota(jnp.int32, shape, axis)


def first_half(shape):
    return iota(shape, 1) % WIDE < CHI


def to_rows(nat, rows_ref, out_ref, column):
    value = nat.astype(F32)
    rows_ref[...] = jnp.concatenate([value, value], axis=0).T
    low = first_half((DD, WIDE))
    for at in range(HALF):
        even = rows_ref[pl.ds(2 * at, DD, stride=CHI), :]
        odd = rows_ref[pl.ds(2 * at + 1, DD, stride=CHI), :]
        out_ref[at * DD : (at + 1) * DD, column : column + WIDE] = jnp.where(low, even, odd).astype(BF)


def from_rows(value, rows_ref):
    for at in range(HALF):
        tile = value[at * DD : (at + 1) * DD, :]
        rows_ref[pl.ds(2 * at, DD, stride=CHI), :] = tile
        rows_ref[pl.ds(2 * at + 1, DD, stride=CHI), :] = tile
    turned = rows_ref[...].T
    even = iota((CHI, ORDER), 1) % 2 == 0
    return jnp.where(even, turned[:CHI], turned[CHI:])


def spread(nat, out_ref, row):
    value = nat.astype(F32)
    low = first_half((CHI, WIDE))
    zero = jnp.zeros((CHI, WIDE), F32)
    for pair in range(DD // 2):
        tile = value[:, pair * WIDE : (pair + 1) * WIDE]
        swapped = pltpu.roll(tile, CHI, 1)
        at = 2 * pair * WIDE
        out_ref[row : row + CHI, at : at + WIDE] = jnp.where(low, tile, zero).astype(BF)
        out_ref[row + CHI : row + WIDE, at : at + WIDE] = jnp.where(low, zero, swapped).astype(BF)
        at = at + WIDE
        out_ref[row : row + CHI, at : at + WIDE] = jnp.where(low, swapped, zero).astype(BF)
        out_ref[row + CHI : row + WIDE, at : at + WIDE] = jnp.where(low, zero, tile).astype(BF)


def gather_pair(value):
    low = first_half((CHI, WIDE))
    even, odd = value[:CHI], value[CHI:]
    stay = jnp.where(low, even[:, :WIDE], odd[:, WIDE:])
    move = jnp.where(low, even[:, WIDE:], odd[:, :WIDE])
    return stay + pltpu.roll(move, CHI, 1)


def leg_maps():
    column = iota((DD, 2 * WIDE), 1)
    small = iota((DD, 2 * WIDE), 0)
    ket_c = ((column // 4) % 4) * 4 + column // 64 == small
    bra_c = (column % 4) * 4 + (column // 16) % 4 == small
    return ket_c.astype(BF), bra_c.astype(BF)


def prepare_kernel(
    site_ref, sketch_hbm, gtop_hbm, gleft_hbm,
    a_ref, ket_ref, bra_ref, cols_ref, turned_ref, gwide_ref,
    rows_ref, sketch_ref, gtop_ref, gleft_ref, sems,
):
    copies = [
        pltpu.make_async_copy(source, target, sems.at[at])
        for at, (source, target) in enumerate(
            ((gtop_hbm, gtop_ref), (sketch_hbm, sketch_ref), (gleft_hbm, gleft_ref))
        )
    ]
    for copy in copies:
        copy.start()
    ket_map, bra_map = leg_maps()
    total = None
    for phys in range(2):
        site = site_ref[phys]
        ket = dot_tn(ket_map, dot_tn(site, ket_map).astype(BF))
        bra = dot_tn(bra_map, dot_tn(site, bra_map).astype(BF))
        ket_ref[phys] = ket.astype(BF)
        bra_ref[phys] = bra.astype(BF)
        total = ket * bra if total is None else total + ket * bra
    a_ref[...] = total.astype(BF)
    copies[0].wait()
    to_rows(gtop_ref[...], rows_ref, cols_ref, 0)
    copies[1].wait()
    to_rows(sketch_ref[...], rows_ref, cols_ref, WIDE)
    turned_ref[...] = cols_ref[...].T
    copies[2].wait()
    spread(gleft_ref[...], gwide_ref, 0)


def corner_pair(corner):
    nothing = jnp.zeros((CHI, CHI), BF)
    return jnp.concatenate(
        [jnp.concatenate([corner, nothing], axis=1), jnp.concatenate([nothing, corner], axis=1)], axis=0
    )


def forward_kernel(
    corner_ref, top_ref, left_ref, a_ref, turned_ref,
    sketched_ref, rightward_ref, tops_ref, first_ref, lwide_ref, second_ref, quad_ref,
    rows_ref,
):
    to_rows(top_ref[...], rows_ref, tops_ref, 0)
    first_ref[...] = dot_nt(tops_ref[...], corner_pair(corner_ref[...])).astype(BF)
    spread(left_ref[...], lwide_ref, 0)

    def second_step(pair, carry):
        at = pl.multiple_of(pair * 2 * WIDE, 2 * WIDE)
        block = dot(first_ref[...], lwide_ref[:, pl.ds(at, 2 * WIDE)]).astype(BF)
        row = pl.multiple_of(pair * 2 * DD, 2 * DD)
        for one in range(HALF):
            piece = block[one * DD : (one + 1) * DD]
            second_ref[pl.ds(row, DD), one * WIDE : (one + 1) * WIDE] = piece[:, :WIDE]
            second_ref[pl.ds(row + DD, DD), one * WIDE : (one + 1) * WIDE] = piece[:, WIDE:]
        return carry

    lax.fori_loop(0, DD // 2, second_step, 0, unroll=2)

    def quad_step(pair, carry):
        at = pl.multiple_of(pair * 2 * WIDE, 2 * WIDE)
        block = dot(a_ref[...], second_ref[:, pl.ds(at, 2 * WIDE)]).astype(BF)
        row = pl.multiple_of(pair * 2 * DD, 2 * DD)
        for leg in range(DD):
            piece = block[leg * DD : (leg + 1) * DD]
            quad_ref[pl.ds(row, DD), leg * WIDE : (leg + 1) * WIDE] = piece[:, :WIDE]
            quad_ref[pl.ds(row + DD, DD), leg * WIDE : (leg + 1) * WIDE] = piece[:, WIDE:]
        return carry

    lax.fori_loop(0, HALF // 2, quad_step, 0, unroll=4)

    for pair in range(DD // 2):
        at = pair * 2 * WIDE
        block = dot(turned_ref[...], quad_ref[:, at : at + 2 * WIDE])
        rightward_ref[:, pair * WIDE : (pair + 1) * WIDE] = gather_pair(block[:WIDE]).astype(BF)
        sketched_ref[:, pair * WIDE : (pair + 1) * WIDE] = gather_pair(block[WIDE:]).astype(BF)


def downward_kernel(quad_ref, gwide_ref, downward_ref, rows_ref):
    down = dot_nt(quad_ref[...], gwide_ref[...])
    downward_ref[...] = from_rows(down, rows_ref).astype(BF)


def partial_kernel(below_ref, beside_ref, cols_ref, gwide_ref, part_ref, rows_ref, right_ref, left_ref):
    to_rows(below_ref[...], rows_ref, right_ref, 0)
    right_ref[:, WIDE:] = cols_ref[:, :WIDE]
    left_ref[:WIDE, :] = gwide_ref[...]
    spread(beside_ref[...], left_ref, WIDE)

    def step(pair, carry):
        at = pl.multiple_of(pair * 2 * WIDE, 2 * WIDE)
        part_ref[:, pl.ds(at, 2 * WIDE)] = dot(right_ref[...], left_ref[:, pl.ds(at, 2 * WIDE)])
        return carry

    lax.fori_loop(0, DD // 2, step, 0, unroll=2)


def backward_kernel(
    above_ref, behind_ref, part_ref, cols_ref, a_ref, first_ref,
    left_out_ref, dquad_ref, dsecond_ref,
    left_ref,
):
    arrived = (above_ref[...].astype(F32) + behind_ref[...].astype(F32)).astype(BF)
    spread(arrived, left_ref, 0)

    def dquad_step(pair, carry):
        at = pl.multiple_of(pair * 2 * WIDE, 2 * WIDE)
        block = dot(cols_ref[:, WIDE:], left_ref[:, pl.ds(at, 2 * WIDE)])
        block = (block + part_ref[:, pl.ds(at, 2 * WIDE)]).astype(BF)
        row = pl.multiple_of(pair * 2 * DD, 2 * DD)
        for one in range(HALF):
            piece = block[one * DD : (one + 1) * DD]
            dquad_ref[pl.ds(row, DD), one * WIDE : (one + 1) * WIDE] = piece[:, :WIDE]
            dquad_ref[pl.ds(row + DD, DD), one * WIDE : (one + 1) * WIDE] = piece[:, WIDE:]
        return carry

    lax.fori_loop(0, DD // 2, dquad_step, 0, unroll=2)
    a_turned = a_ref[...].T

    def dsecond_step(pair, carry):
        at = pl.multiple_of(pair * 2 * WIDE, 2 * WIDE)
        block = dot(a_turned, dquad_ref[:, pl.ds(at, 2 * WIDE)]).astype(BF)
        row = pl.multiple_of(pair * 2 * DD, 2 * DD)
        for leg in range(DD):
            piece = block[leg * DD : (leg + 1) * DD]
            dsecond_ref[pl.ds(row, DD), leg * WIDE : (leg + 1) * WIDE] = piece[:, :WIDE]
            dsecond_ref[pl.ds(row + DD, DD), leg * WIDE : (leg + 1) * WIDE] = piece[:, WIDE:]
        return carry

    lax.fori_loop(0, HALF // 2, dsecond_step, 0, unroll=4)

    first_turned = first_ref[...].T
    for pair in range(DD // 2):
        at = pair * 2 * WIDE
        block = dot(first_turned, dsecond_ref[:, at : at + 2 * WIDE])
        left_out_ref[:, pair * WIDE : (pair + 1) * WIDE] = gather_pair(block).astype(BF)


def edges_kernel(dsecond_ref, lwide_ref, tops_ref, corner_ref, top_out_ref, corner_out_ref, rows_ref):
    dfirst = dot_nt(dsecond_ref[...], lwide_ref[...]).astype(BF)
    dtop = dot(dfirst, corner_pair(corner_ref[...]))
    top_out_ref[...] = from_rows(dtop, rows_ref).astype(BF)
    dcorner = dot_tn(dfirst, tops_ref[...])
    corner_out_ref[...] = (dcorner[:CHI, :CHI] + pltpu.roll(dcorner[CHI:], CHI, 1)[:, :CHI]).astype(BF)


def split(value):
    high = value.astype(BF)
    return high, (value - high.astype(F32)).astype(BF)


def site_kernel(dquad_ref, second_ref, ket_ref, bra_ref, out_ref):
    grad = dot_nt(dquad_ref[...], second_ref[...])
    ket_map, bra_map = leg_maps()
    for phys in range(2):
        total = None
        for other_ref, leg_map in ((ket_ref, bra_map), (bra_ref, ket_map)):
            for part in split(grad * other_ref[phys].astype(F32)):
                half = dot_nt(leg_map, part)
                for piece in split(half):
                    term = dot_nt(piece, leg_map)
                    total = term if total is None else total + term
        out_ref[phys] = total


def finish_kernel(corner_ref, top_ref, left_ref, corner_hbm, top_hbm, left_hbm, sems):
    copies = [
        pltpu.make_async_copy(source, target, sems.at[at])
        for at, (source, target) in enumerate(
            ((left_ref, left_hbm), (top_ref, top_hbm), (corner_ref, corner_hbm))
        )
    ]
    for copy in copies:
        copy.start()
    for copy in copies:
        copy.wait()


def shape(*dims, dtype=BF):
    return jax.ShapeDtypeStruct(dims, dtype)


def call(kernel, outs, scratch, flops, moved, specs=None, out_specs=None, room=20 << 20):
    extra = {} if specs is None else {"in_specs": specs}
    if out_specs is not None:
        extra["out_specs"] = out_specs
    return pl.pallas_call(
        kernel,
        out_shape=outs,
        **extra,
        scratch_shapes=scratch,
        compiler_params=pltpu.CompilerParams(vmem_limit_bytes=room),
        cost_estimate=pl.CostEstimate(flops=flops, bytes_accessed=moved, transcendentals=0),
    )


def from_behind(value, down, right):
    rows, columns = lax.axis_size("row"), lax.axis_size("col")
    pairs = [
        (i * columns + j, (i + down) % rows * columns + (j + right) % columns)
        for i in range(rows)
        for j in range(columns)
    ]
    return lax.ppermute(value, ("row", "col"), pairs)


def step(corner, top_edge, left_edge, site_tensor, sketch, grad_left, grad_top):
    site = site_tensor.reshape(2, DD, DD)
    left_used = from_behind(left_edge[0, 0], 0, 1)
    top_used = from_behind(top_edge[0, 0], 1, 0)
    corner_used = from_behind(corner[0, 0], 1, 1)
    rows = pltpu.VMEM((ORDER, WIDE), F32)
    edge = pltpu.VMEM((CHI, ORDER), BF)
    here = pl.BlockSpec(memory_space=pltpu.HBM)
    a_mat, ket, bra, cols, turned, gwide = call(
        prepare_kernel,
        (
            shape(256, 256), shape(2, 256, 256), shape(2, 256, 256), shape(512, 256), shape(256, 512), shape(128, 2048),
        ),
        [rows, edge, edge, edge, pltpu.SemaphoreType.DMA((3,))],
        10**7, 2 * 10**6,
        [pl.BlockSpec(memory_space=pltpu.VMEM), here, here, here],
        room=PREP,
    )(site, sketch[0, 0], grad_top[0, 0], grad_left[0, 0])
    sketched, rightward, tops, first, lwide, second, quad = call(
        forward_kernel,
        (
            shape(CHI, ORDER), shape(CHI, ORDER),
            shape(512, WIDE), shape(512, WIDE), shape(WIDE, 2048), shape(256, 4096), shape(512, 2048),
        ),
        [rows],
        2 * 10**9, 4 * 10**6,
    )(corner_used, top_used, left_used, a_mat, turned)
    sketch_beside = from_behind(sketched, 0, -1)
    sketch_below = from_behind(sketched, -1, 0)
    from_left = from_behind(rightward, 0, 1)
    downward = call(downward_kernel, shape(CHI, ORDER), [rows], 3 * 10**8, 3 * 10**6)(quad, gwide)
    from_above = from_behind(downward, 1, 0)
    part = call(
        partial_kernel, shape(512, 2048, dtype=F32),
        [rows, pltpu.VMEM((512, 256), BF), pltpu.VMEM((256, 2048), BF)],
        5 * 10**8, 5 * 10**6,
    )(sketch_below, sketch_beside, cols, gwide)
    grad_lefted, dquad, dsecond = call(
        backward_kernel,
        (shape(CHI, ORDER), shape(256, 4096), shape(512, 2048)),
        [pltpu.VMEM((128, 2048), BF)],
        2 * 10**9, 8 * 10**6,
    )(from_above, from_left, part, cols, a_mat, first)
    left_result = from_behind(grad_lefted, 0, -1)
    grad_topped, grad_cornered = call(
        edges_kernel, (shape(CHI, ORDER), shape(CHI, CHI)), [rows], 3 * 10**8, 3 * 10**6
    )(dsecond, lwide, tops, corner_used)
    top_result = from_behind(grad_topped, -1, 0)
    corner_result = from_behind(grad_cornered, -1, -1)
    site_result = call(site_kernel, shape(2, DD, DD, dtype=F32), [], 10**9, 5 * 10**6)(dquad, second, ket, bra)
    corner_result, top_result, left_result = call(
        finish_kernel,
        (shape(CHI, CHI), shape(CHI, ORDER), shape(CHI, ORDER)),
        [pltpu.SemaphoreType.DMA((3,))],
        0, 6 * 10**5,
        [pl.BlockSpec(memory_space=pltpu.VMEM)] * 3,
        (here, here, here),
    )(corner_result, top_result, left_result)
    return (
        corner_result[None, None],
        top_result[None, None],
        left_result[None, None],
        site_result.reshape(site_tensor.shape),
    )


def solution(mesh):
    flat = P("row", "col", None, None)
    deep = P("row", "col", None, None, None, None, None)
    return jax.shard_map(
        step,
        mesh=mesh,
        in_specs=(flat, flat, flat, deep, flat, flat, flat),
        out_specs=(flat, flat, flat, deep),
        check_vma=False,
    )
```

```python
import jax
import jax.numpy as jnp
from jax import lax
from jax.experimental import pallas as pl
from jax.experimental.pallas import tpu as pltpu
from jax.sharding import PartitionSpec as P


BF = jnp.bfloat16
F32 = jnp.float32
CHI = 64
DD = 16
ORDER = DD * CHI
HALF = CHI // 2
WIDE = 2 * CHI
PREP = 20 << 20


def dot(lhs, rhs):
    return jnp.dot(lhs, rhs, preferred_element_type=F32)


def dot_nt(lhs, rhs):
    return lax.dot_general(lhs, rhs, (((1,), (1,)), ((), ())), preferred_element_type=F32)


def dot_tn(lhs, rhs):
    return lax.dot_general(lhs, rhs, (((0,), (0,)), ((), ())), preferred_element_type=F32)


def iota(shape, axis):
    return lax.broadcasted_iota(jnp.int32, shape, axis)


def first_half(shape):
    return iota(shape, 1) % WIDE < CHI


def to_rows(nat, rows_ref, out_ref, column):
    rows_ref[...] = jnp.concatenate([nat, nat], axis=0).T.astype(F32)
    low = first_half((DD, WIDE))
    for at in range(HALF):
        even = rows_ref[pl.ds(2 * at, DD, stride=CHI), :]
        odd = rows_ref[pl.ds(2 * at + 1, DD, stride=CHI), :]
        out_ref[at * DD : (at + 1) * DD, column : column + WIDE] = jnp.where(low, even, odd).astype(BF)


def from_rows(value, rows_ref):
    for at in range(HALF):
        tile = value[at * DD : (at + 1) * DD, :]
        rows_ref[pl.ds(2 * at, DD, stride=CHI), :] = tile
        rows_ref[pl.ds(2 * at + 1, DD, stride=CHI), :] = tile
    turned = rows_ref[...].astype(BF).T
    even = iota((CHI, ORDER), 1) % 2 == 0
    return jnp.where(even, turned[:CHI], turned[CHI:])


def spread(nat, out_ref, row):
    value = nat.astype(F32)
    low = first_half((CHI, WIDE))
    zero = jnp.zeros((CHI, WIDE), F32)
    for pair in range(DD // 2):
        tile = value[:, pair * WIDE : (pair + 1) * WIDE]
        swapped = pltpu.roll(tile, CHI, 1)
        at = 2 * pair * WIDE
        out_ref[row : row + CHI, at : at + WIDE] = jnp.where(low, tile, zero).astype(BF)
        out_ref[row + CHI : row + WIDE, at : at + WIDE] = jnp.where(low, zero, swapped).astype(BF)
        at = at + WIDE
        out_ref[row : row + CHI, at : at + WIDE] = jnp.where(low, swapped, zero).astype(BF)
        out_ref[row + CHI : row + WIDE, at : at + WIDE] = jnp.where(low, zero, tile).astype(BF)


def gather_pair(value):
    low = first_half((CHI, WIDE))
    even, odd = value[:CHI], value[CHI:]
    stay = jnp.where(low, even[:, :WIDE], odd[:, WIDE:])
    move = jnp.where(low, even[:, WIDE:], odd[:, :WIDE])
    return stay + pltpu.roll(move, CHI, 1)


def leg_maps():
    column = iota((DD, 2 * WIDE), 1)
    small = iota((DD, 2 * WIDE), 0)
    ket_c = ((column // 4) % 4) * 4 + column // 64 == small
    bra_c = (column % 4) * 4 + (column // 16) % 4 == small
    return ket_c.astype(BF), bra_c.astype(BF)


def prepare_kernel(
    site_ref, sketch_hbm, gtop_hbm, gleft_hbm,
    a_ref, ket_ref, bra_ref, cols_ref, turned_ref, gwide_ref,
    rows_ref, sketch_ref, gtop_ref, gleft_ref, sems,
):
    copies = [
        pltpu.make_async_copy(source, target, sems.at[at])
        for at, (source, target) in enumerate(
            ((gtop_hbm, gtop_ref), (sketch_hbm, sketch_ref), (gleft_hbm, gleft_ref))
        )
    ]
    for copy in copies:
        copy.start()
    ket_map, bra_map = leg_maps()
    total = None
    for phys in range(2):
        site = site_ref[phys]
        ket = dot_tn(ket_map, dot_tn(site, ket_map).astype(BF))
        bra = dot_tn(bra_map, dot_tn(site, bra_map).astype(BF))
        ket_ref[phys] = ket.astype(BF)
        bra_ref[phys] = bra.astype(BF)
        total = ket * bra if total is None else total + ket * bra
    a_ref[...] = total.astype(BF)
    copies[0].wait()
    to_rows(gtop_ref[...], rows_ref, cols_ref, 0)
    copies[1].wait()
    to_rows(sketch_ref[...], rows_ref, cols_ref, WIDE)
    turned_ref[...] = cols_ref[...].T
    copies[2].wait()
    spread(gleft_ref[...], gwide_ref, 0)


def corner_pair(corner):
    nothing = jnp.zeros((CHI, CHI), BF)
    return jnp.concatenate(
        [jnp.concatenate([corner, nothing], axis=1), jnp.concatenate([nothing, corner], axis=1)], axis=0
    )


def forward_kernel(
    corner_ref, top_ref, left_ref, a_ref, turned_ref,
    sketched_ref, rightward_ref, tops_ref, first_ref, lwide_ref, second_ref, quad_ref,
    rows_ref,
):
    to_rows(top_ref[...], rows_ref, tops_ref, 0)
    first_ref[...] = dot_nt(tops_ref[...], corner_pair(corner_ref[...])).astype(BF)
    spread(left_ref[...], lwide_ref, 0)

    def second_step(pair, carry):
        at = pl.multiple_of(pair * 2 * WIDE, 2 * WIDE)
        block = dot(first_ref[...], lwide_ref[:, pl.ds(at, 2 * WIDE)]).astype(BF)
        row = pl.multiple_of(pair * 2 * DD, 2 * DD)
        for one in range(HALF):
            piece = block[one * DD : (one + 1) * DD]
            second_ref[pl.ds(row, DD), one * WIDE : (one + 1) * WIDE] = piece[:, :WIDE]
            second_ref[pl.ds(row + DD, DD), one * WIDE : (one + 1) * WIDE] = piece[:, WIDE:]
        return carry

    lax.fori_loop(0, DD // 2, second_step, 0, unroll=8)

    def quad_step(pair, carry):
        at = pl.multiple_of(pair * 2 * WIDE, 2 * WIDE)
        block = dot(a_ref[...], second_ref[:, pl.ds(at, 2 * WIDE)]).astype(BF)
        row = pl.multiple_of(pair * 2 * DD, 2 * DD)
        for leg in range(DD):
            piece = block[leg * DD : (leg + 1) * DD]
            quad_ref[pl.ds(row, DD), leg * WIDE : (leg + 1) * WIDE] = piece[:, :WIDE]
            quad_ref[pl.ds(row + DD, DD), leg * WIDE : (leg + 1) * WIDE] = piece[:, WIDE:]
        return carry

    lax.fori_loop(0, HALF // 2, quad_step, 0, unroll=16)

    for pair in range(DD // 2):
        at = pair * 2 * WIDE
        block = dot(turned_ref[...], quad_ref[:, at : at + 2 * WIDE])
        rightward_ref[:, pair * WIDE : (pair + 1) * WIDE] = gather_pair(block[:WIDE]).astype(BF)
        sketched_ref[:, pair * WIDE : (pair + 1) * WIDE] = gather_pair(block[WIDE:]).astype(BF)


def downward_kernel(quad_ref, gwide_ref, downward_ref, rows_ref):
    down = dot_nt(quad_ref[...], gwide_ref[...])
    downward_ref[...] = from_rows(down, rows_ref)


def partial_kernel(below_ref, beside_ref, cols_ref, gwide_ref, part_ref, rows_ref, right_ref, left_ref):
    to_rows(below_ref[...], rows_ref, right_ref, 0)
    right_ref[:, WIDE:] = cols_ref[:, :WIDE]
    left_ref[:WIDE, :] = gwide_ref[...]
    spread(beside_ref[...], left_ref, WIDE)

    def step(pair, carry):
        at = pl.multiple_of(pair * 2 * WIDE, 2 * WIDE)
        part_ref[:, pl.ds(at, 2 * WIDE)] = dot(right_ref[...], left_ref[:, pl.ds(at, 2 * WIDE)])
        return carry

    lax.fori_loop(0, DD // 2, step, 0, unroll=8)


def backward_kernel(
    above_ref, behind_ref, part_ref, cols_ref, a_ref, first_ref,
    left_out_ref, dquad_ref, dsecond_ref,
    left_ref,
):
    arrived = (above_ref[...].astype(F32) + behind_ref[...].astype(F32)).astype(BF)
    spread(arrived, left_ref, 0)

    def dquad_step(pair, carry):
        at = pl.multiple_of(pair * 2 * WIDE, 2 * WIDE)
        block = dot(cols_ref[:, WIDE:], left_ref[:, pl.ds(at, 2 * WIDE)])
        block = (block + part_ref[:, pl.ds(at, 2 * WIDE)]).astype(BF)
        row = pl.multiple_of(pair * 2 * DD, 2 * DD)
        for one in range(HALF):
            piece = block[one * DD : (one + 1) * DD]
            dquad_ref[pl.ds(row, DD), one * WIDE : (one + 1) * WIDE] = piece[:, :WIDE]
            dquad_ref[pl.ds(row + DD, DD), one * WIDE : (one + 1) * WIDE] = piece[:, WIDE:]
        return carry

    lax.fori_loop(0, DD // 2, dquad_step, 0, unroll=8)
    a_turned = a_ref[...].T

    def dsecond_step(pair, carry):
        at = pl.multiple_of(pair * 2 * WIDE, 2 * WIDE)
        block = dot(a_turned, dquad_ref[:, pl.ds(at, 2 * WIDE)]).astype(BF)
        row = pl.multiple_of(pair * 2 * DD, 2 * DD)
        for leg in range(DD):
            piece = block[leg * DD : (leg + 1) * DD]
            dsecond_ref[pl.ds(row, DD), leg * WIDE : (leg + 1) * WIDE] = piece[:, :WIDE]
            dsecond_ref[pl.ds(row + DD, DD), leg * WIDE : (leg + 1) * WIDE] = piece[:, WIDE:]
        return carry

    lax.fori_loop(0, HALF // 2, dsecond_step, 0, unroll=16)

    first_turned = first_ref[...].T
    for pair in range(DD // 2):
        at = pair * 2 * WIDE
        block = dot(first_turned, dsecond_ref[:, at : at + 2 * WIDE])
        left_out_ref[:, pair * WIDE : (pair + 1) * WIDE] = gather_pair(block).astype(BF)


def edges_kernel(dsecond_ref, lwide_ref, tops_ref, corner_ref, top_out_ref, corner_out_ref, rows_ref):
    dfirst = dot_nt(dsecond_ref[...], lwide_ref[...]).astype(BF)
    dtop = dot(dfirst, corner_pair(corner_ref[...]))
    top_out_ref[...] = from_rows(dtop, rows_ref)
    dcorner = dot_tn(dfirst, tops_ref[...])
    corner_out_ref[...] = (dcorner[:CHI, :CHI] + pltpu.roll(dcorner[CHI:], CHI, 1)[:, :CHI]).astype(BF)


def site_kernel(dquad_ref, second_ref, ket_ref, bra_ref, out_ref):
    grad = dot_nt(dquad_ref[...], second_ref[...])
    ket_map, bra_map = leg_maps()
    total = None
    for other_ref, leg_map in ((ket_ref, bra_map), (bra_ref, ket_map)):
        pieces = [(grad * other_ref[phys].astype(F32)).astype(BF) for phys in range(2)]
        half = dot_nt(jnp.concatenate(pieces, axis=0), leg_map).astype(BF)
        term = dot(leg_map, jnp.concatenate([half[: 2 * WIDE], half[2 * WIDE :]], axis=1))
        total = term if total is None else total + term
    turned = total.T
    out_ref[0] = turned[:DD]
    out_ref[1] = turned[DD:]


def finish_kernel(corner_ref, top_ref, left_ref, corner_hbm, top_hbm, left_hbm, sems):
    copies = [
        pltpu.make_async_copy(source, target, sems.at[at])
        for at, (source, target) in enumerate(
            ((left_ref, left_hbm), (top_ref, top_hbm), (corner_ref, corner_hbm))
        )
    ]
    for copy in copies:
        copy.start()
    for copy in copies:
        copy.wait()


def shape(*dims, dtype=BF):
    return jax.ShapeDtypeStruct(dims, dtype)


def call(kernel, outs, scratch, flops, moved, specs=None, out_specs=None, room=20 << 20):
    extra = {} if specs is None else {"in_specs": specs}
    if out_specs is not None:
        extra["out_specs"] = out_specs
    return pl.pallas_call(
        kernel,
        out_shape=outs,
        **extra,
        scratch_shapes=scratch,
        compiler_params=pltpu.CompilerParams(vmem_limit_bytes=room),
        cost_estimate=pl.CostEstimate(flops=flops, bytes_accessed=moved, transcendentals=0),
    )


def in_hbm(shard):
    return pltpu.with_memory_space_constraint(shard[0, 0], pltpu.HBM)


def from_behind(value, down, right):
    rows, columns = lax.axis_size("row"), lax.axis_size("col")
    pairs = [
        (i * columns + j, (i + down) % rows * columns + (j + right) % columns)
        for i in range(rows)
        for j in range(columns)
    ]
    return lax.ppermute(value, ("row", "col"), pairs)


def step(corner, top_edge, left_edge, site_tensor, sketch, grad_left, grad_top):
    site = site_tensor.reshape(2, DD, DD)
    left_used = from_behind(left_edge[0, 0], 0, 1)
    top_used = from_behind(top_edge[0, 0], 1, 0)
    corner_used = from_behind(corner[0, 0], 1, 1)
    rows = pltpu.VMEM((ORDER, WIDE), F32)
    edge = pltpu.VMEM((CHI, ORDER), BF)
    here = pl.BlockSpec(memory_space=pltpu.HBM)
    a_mat, ket, bra, cols, turned, gwide = call(
        prepare_kernel,
        (
            shape(256, 256), shape(2, 256, 256), shape(2, 256, 256), shape(512, 256), shape(256, 512), shape(128, 2048),
        ),
        [rows, edge, edge, edge, pltpu.SemaphoreType.DMA((3,))],
        10**7, 2 * 10**6,
        [pl.BlockSpec(memory_space=pltpu.VMEM), here, here, here],
        room=PREP,
    )(site, in_hbm(sketch), in_hbm(grad_top), in_hbm(grad_left))
    sketched, rightward, tops, first, lwide, second, quad = call(
        forward_kernel,
        (
            shape(CHI, ORDER), shape(CHI, ORDER),
            shape(512, WIDE), shape(512, WIDE), shape(WIDE, 2048), shape(256, 4096), shape(512, 2048),
        ),
        [rows],
        2 * 10**9, 4 * 10**6,
    )(corner_used, top_used, left_used, a_mat, turned)
    sketch_beside = from_behind(sketched, 0, -1)
    sketch_below = from_behind(sketched, -1, 0)
    from_left = from_behind(rightward, 0, 1)
    downward = call(downward_kernel, shape(CHI, ORDER), [rows], 3 * 10**8, 3 * 10**6)(quad, gwide)
    from_above = from_behind(downward, 1, 0)
    part = call(
        partial_kernel, shape(512, 2048, dtype=F32),
        [rows, pltpu.VMEM((512, 256), BF), pltpu.VMEM((256, 2048), BF)],
        5 * 10**8, 5 * 10**6,
    )(sketch_below, sketch_beside, cols, gwide)
    grad_lefted, dquad, dsecond = call(
        backward_kernel,
        (shape(CHI, ORDER), shape(256, 4096), shape(512, 2048)),
        [pltpu.VMEM((128, 2048), BF)],
        2 * 10**9, 8 * 10**6,
    )(from_above, from_left, part, cols, a_mat, first)
    left_result = from_behind(grad_lefted, 0, -1)
    grad_topped, grad_cornered = call(
        edges_kernel, (shape(CHI, ORDER), shape(CHI, CHI)), [rows], 3 * 10**8, 3 * 10**6
    )(dsecond, lwide, tops, corner_used)
    top_result = from_behind(grad_topped, -1, 0)
    corner_result = from_behind(grad_cornered, -1, -1)
    site_result = call(site_kernel, shape(2, DD, DD, dtype=F32), [], 10**9, 5 * 10**6)(dquad, second, ket, bra)
    corner_result, top_result, left_result = call(
        finish_kernel,
        (shape(CHI, CHI), shape(CHI, ORDER), shape(CHI, ORDER)),
        [pltpu.SemaphoreType.DMA((3,))],
        0, 6 * 10**5,
        [pl.BlockSpec(memory_space=pltpu.VMEM)] * 3,
        (here, here, here),
    )(corner_result, top_result, left_result)
    return (
        corner_result[None, None],
        top_result[None, None],
        left_result[None, None],
        site_result.reshape(site_tensor.shape),
    )


def solution(mesh):
    flat = P("row", "col", None, None)
    deep = P("row", "col", None, None, None, None, None)
    return jax.shard_map(
        step,
        mesh=mesh,
        in_specs=(flat, flat, flat, deep, flat, flat, flat),
        out_specs=(flat, flat, flat, deep),
        check_vma=False,
    )
```

```python
import jax
import jax.numpy as jnp
from jax import lax
from jax.experimental import pallas as pl
from jax.experimental.pallas import tpu as pltpu
from jax.sharding import PartitionSpec as P


BF = jnp.bfloat16
F32 = jnp.float32
CHI = 64
DD = 16
ORDER = DD * CHI
HALF = CHI // 2
WIDE = 2 * CHI
LEAP = DD + 1
PREP = 20 << 20


def dot(lhs, rhs):
    return jnp.dot(lhs, rhs, preferred_element_type=F32)


def dot_nt(lhs, rhs):
    return lax.dot_general(lhs, rhs, (((1,), (1,)), ((), ())), preferred_element_type=F32)


def dot_tn(lhs, rhs):
    return lax.dot_general(lhs, rhs, (((0,), (0,)), ((), ())), preferred_element_type=F32)


def iota(shape, axis):
    return lax.broadcasted_iota(jnp.int32, shape, axis)


def first_half(shape):
    return iota(shape, 1) % WIDE < CHI


def to_rows(nat, rows_ref, out_ref, column):
    turned = jnp.concatenate([nat, nat], axis=0).T.astype(F32)
    for leg in range(DD):
        rows_ref[pl.ds(leg, CHI, stride=LEAP), :] = turned[leg * CHI : (leg + 1) * CHI]
    low = first_half((DD, WIDE))
    for at in range(HALF):
        even = rows_ref[2 * at * LEAP : 2 * at * LEAP + DD, :]
        odd = rows_ref[(2 * at + 1) * LEAP : (2 * at + 1) * LEAP + DD, :]
        out_ref[at * DD : (at + 1) * DD, column : column + WIDE] = jnp.where(low, even, odd).astype(BF)


def from_rows(value, rows_ref):
    for at in range(HALF):
        tile = value[at * DD : (at + 1) * DD, :]
        rows_ref[2 * at * LEAP : 2 * at * LEAP + DD, :] = tile
        rows_ref[(2 * at + 1) * LEAP : (2 * at + 1) * LEAP + DD, :] = tile
    legs = [rows_ref[pl.ds(leg, CHI, stride=LEAP), :].astype(BF) for leg in range(DD)]
    turned = jnp.concatenate(legs, axis=0).T
    even = iota((CHI, ORDER), 1) % 2 == 0
    return jnp.where(even, turned[:CHI], turned[CHI:])


def spread(nat, out_ref, row):
    value = nat.astype(F32)
    low = first_half((CHI, WIDE))
    zero = jnp.zeros((CHI, WIDE), F32)
    for pair in range(DD // 2):
        tile = value[:, pair * WIDE : (pair + 1) * WIDE]
        swapped = pltpu.roll(tile, CHI, 1)
        at = 2 * pair * WIDE
        out_ref[row : row + CHI, at : at + WIDE] = jnp.where(low, tile, zero).astype(BF)
        out_ref[row + CHI : row + WIDE, at : at + WIDE] = jnp.where(low, zero, swapped).astype(BF)
        at = at + WIDE
        out_ref[row : row + CHI, at : at + WIDE] = jnp.where(low, swapped, zero).astype(BF)
        out_ref[row + CHI : row + WIDE, at : at + WIDE] = jnp.where(low, zero, tile).astype(BF)


def gather_pair(value):
    low = first_half((CHI, WIDE))
    even, odd = value[:CHI], value[CHI:]
    stay = jnp.where(low, even[:, :WIDE], odd[:, WIDE:])
    move = jnp.where(low, even[:, WIDE:], odd[:, :WIDE])
    return stay + pltpu.roll(move, CHI, 1)


def leg_maps():
    column = iota((DD, 2 * WIDE), 1)
    small = iota((DD, 2 * WIDE), 0)
    ket_c = ((column // 4) % 4) * 4 + column // 64 == small
    bra_c = (column % 4) * 4 + (column // 16) % 4 == small
    return ket_c.astype(BF), bra_c.astype(BF)


def prepare_kernel(
    site_ref, sketch_hbm, gtop_hbm, gleft_hbm,
    a_ref, ket_ref, bra_ref, cols_ref, turned_ref, gwide_ref,
    rows_ref, sketch_ref, gtop_ref, gleft_ref, sems,
):
    copies = [
        pltpu.make_async_copy(source, target, sems.at[at])
        for at, (source, target) in enumerate(
            ((gtop_hbm, gtop_ref), (sketch_hbm, sketch_ref), (gleft_hbm, gleft_ref))
        )
    ]
    for copy in copies:
        copy.start()
    ket_map, bra_map = leg_maps()
    total = None
    for phys in range(2):
        site = site_ref[phys]
        ket = dot_tn(ket_map, dot_tn(site, ket_map).astype(BF))
        bra = dot_tn(bra_map, dot_tn(site, bra_map).astype(BF))
        ket_ref[phys] = ket.astype(BF)
        bra_ref[phys] = bra.astype(BF)
        total = ket * bra if total is None else total + ket * bra
    a_ref[...] = total.astype(BF)
    copies[0].wait()
    to_rows(gtop_ref[...], rows_ref, cols_ref, 0)
    copies[1].wait()
    to_rows(sketch_ref[...], rows_ref, cols_ref, WIDE)
    turned_ref[...] = cols_ref[...].T
    copies[2].wait()
    spread(gleft_ref[...], gwide_ref, 0)


def corner_pair(corner):
    nothing = jnp.zeros((CHI, CHI), BF)
    return jnp.concatenate(
        [jnp.concatenate([corner, nothing], axis=1), jnp.concatenate([nothing, corner], axis=1)], axis=0
    )


def forward_kernel(
    corner_ref, top_ref, left_ref, a_ref, turned_ref,
    sketched_ref, rightward_ref, tops_ref, first_ref, lwide_ref, second_ref, quad_ref,
    rows_ref,
):
    to_rows(top_ref[...], rows_ref, tops_ref, 0)
    first_ref[...] = dot_nt(tops_ref[...], corner_pair(corner_ref[...])).astype(BF)
    spread(left_ref[...], lwide_ref, 0)

    def second_step(pair, carry):
        at = pl.multiple_of(pair * 2 * WIDE, 2 * WIDE)
        block = dot(first_ref[...], lwide_ref[:, pl.ds(at, 2 * WIDE)]).astype(BF)
        row = pl.multiple_of(pair * 2 * DD, 2 * DD)
        for one in range(HALF):
            piece = block[one * DD : (one + 1) * DD]
            second_ref[pl.ds(row, DD), one * WIDE : (one + 1) * WIDE] = piece[:, :WIDE]
            second_ref[pl.ds(row + DD, DD), one * WIDE : (one + 1) * WIDE] = piece[:, WIDE:]
        return carry

    lax.fori_loop(0, DD // 2, second_step, 0, unroll=8)

    def quad_step(pair, carry):
        at = pl.multiple_of(pair * 2 * WIDE, 2 * WIDE)
        block = dot(a_ref[...], second_ref[:, pl.ds(at, 2 * WIDE)]).astype(BF)
        row = pl.multiple_of(pair * 2 * DD, 2 * DD)
        for leg in range(DD):
            piece = block[leg * DD : (leg + 1) * DD]
            quad_ref[pl.ds(row, DD), leg * WIDE : (leg + 1) * WIDE] = piece[:, :WIDE]
            quad_ref[pl.ds(row + DD, DD), leg * WIDE : (leg + 1) * WIDE] = piece[:, WIDE:]
        return carry

    lax.fori_loop(0, HALF // 2, quad_step, 0, unroll=16)

    for pair in range(DD // 2):
        at = pair * 2 * WIDE
        block = dot(turned_ref[...], quad_ref[:, at : at + 2 * WIDE])
        rightward_ref[:, pair * WIDE : (pair + 1) * WIDE] = gather_pair(block[:WIDE]).astype(BF)
        sketched_ref[:, pair * WIDE : (pair + 1) * WIDE] = gather_pair(block[WIDE:]).astype(BF)


def downward_kernel(quad_ref, gwide_ref, downward_ref, rows_ref):
    down = dot_nt(quad_ref[...], gwide_ref[...])
    downward_ref[...] = from_rows(down, rows_ref)


def partial_kernel(below_ref, beside_ref, cols_ref, gwide_ref, part_ref, rows_ref, right_ref, left_ref):
    to_rows(below_ref[...], rows_ref, right_ref, 0)
    right_ref[:, WIDE:] = cols_ref[:, :WIDE]
    left_ref[:WIDE, :] = gwide_ref[...]
    spread(beside_ref[...], left_ref, WIDE)

    def step(pair, carry):
        at = pl.multiple_of(pair * 2 * WIDE, 2 * WIDE)
        part_ref[:, pl.ds(at, 2 * WIDE)] = dot(right_ref[...], left_ref[:, pl.ds(at, 2 * WIDE)])
        return carry

    lax.fori_loop(0, DD // 2, step, 0, unroll=8)


def backward_kernel(
    above_ref, behind_ref, part_ref, cols_ref, a_ref, first_ref,
    left_out_ref, dquad_ref, dsecond_ref,
    left_ref,
):
    arrived = (above_ref[...].astype(F32) + behind_ref[...].astype(F32)).astype(BF)
    spread(arrived, left_ref, 0)

    def dquad_step(pair, carry):
        at = pl.multiple_of(pair * 2 * WIDE, 2 * WIDE)
        block = dot(cols_ref[:, WIDE:], left_ref[:, pl.ds(at, 2 * WIDE)])
        block = (block + part_ref[:, pl.ds(at, 2 * WIDE)]).astype(BF)
        row = pl.multiple_of(pair * 2 * DD, 2 * DD)
        for one in range(HALF):
            piece = block[one * DD : (one + 1) * DD]
            dquad_ref[pl.ds(row, DD), one * WIDE : (one + 1) * WIDE] = piece[:, :WIDE]
            dquad_ref[pl.ds(row + DD, DD), one * WIDE : (one + 1) * WIDE] = piece[:, WIDE:]
        return carry

    lax.fori_loop(0, DD // 2, dquad_step, 0, unroll=8)
    a_turned = a_ref[...].T

    def dsecond_step(pair, carry):
        at = pl.multiple_of(pair * 2 * WIDE, 2 * WIDE)
        block = dot(a_turned, dquad_ref[:, pl.ds(at, 2 * WIDE)]).astype(BF)
        row = pl.multiple_of(pair * 2 * DD, 2 * DD)
        for leg in range(DD):
            piece = block[leg * DD : (leg + 1) * DD]
            dsecond_ref[pl.ds(row, DD), leg * WIDE : (leg + 1) * WIDE] = piece[:, :WIDE]
            dsecond_ref[pl.ds(row + DD, DD), leg * WIDE : (leg + 1) * WIDE] = piece[:, WIDE:]
        return carry

    lax.fori_loop(0, HALF // 2, dsecond_step, 0, unroll=16)

    first_turned = first_ref[...].T
    for pair in range(DD // 2):
        at = pair * 2 * WIDE
        block = dot(first_turned, dsecond_ref[:, at : at + 2 * WIDE])
        left_out_ref[:, pair * WIDE : (pair + 1) * WIDE] = gather_pair(block).astype(BF)


def edges_kernel(dsecond_ref, lwide_ref, tops_ref, corner_ref, top_out_ref, corner_out_ref, rows_ref):
    dfirst = dot_nt(dsecond_ref[...], lwide_ref[...]).astype(BF)
    dtop = dot(dfirst, corner_pair(corner_ref[...]))
    top_out_ref[...] = from_rows(dtop, rows_ref)
    dcorner = dot_tn(dfirst, tops_ref[...])
    corner_out_ref[...] = (dcorner[:CHI, :CHI] + pltpu.roll(dcorner[CHI:], CHI, 1)[:, :CHI]).astype(BF)


def site_kernel(dquad_ref, second_ref, ket_ref, bra_ref, out_ref):
    grad = dot_nt(dquad_ref[...], second_ref[...])
    ket_map, bra_map = leg_maps()
    total = None
    for other_ref, leg_map in ((ket_ref, bra_map), (bra_ref, ket_map)):
        pieces = [(grad * other_ref[phys].astype(F32)).astype(BF) for phys in range(2)]
        half = dot_nt(jnp.concatenate(pieces, axis=0), leg_map).astype(BF)
        term = dot(leg_map, jnp.concatenate([half[: 2 * WIDE], half[2 * WIDE :]], axis=1))
        total = term if total is None else total + term
    turned = total.T
    out_ref[0] = turned[:DD]
    out_ref[1] = turned[DD:]


def finish_kernel(corner_ref, top_ref, left_ref, corner_hbm, top_hbm, left_hbm, sems):
    copies = [
        pltpu.make_async_copy(source, target, sems.at[at])
        for at, (source, target) in enumerate(
            ((left_ref, left_hbm), (top_ref, top_hbm), (corner_ref, corner_hbm))
        )
    ]
    for copy in copies:
        copy.start()
    for copy in copies:
        copy.wait()


def shape(*dims, dtype=BF):
    return jax.ShapeDtypeStruct(dims, dtype)


def call(kernel, outs, scratch, flops, moved, specs=None, out_specs=None, room=20 << 20):
    extra = {} if specs is None else {"in_specs": specs}
    if out_specs is not None:
        extra["out_specs"] = out_specs
    return pl.pallas_call(
        kernel,
        out_shape=outs,
        **extra,
        scratch_shapes=scratch,
        compiler_params=pltpu.CompilerParams(vmem_limit_bytes=room),
        cost_estimate=pl.CostEstimate(flops=flops, bytes_accessed=moved, transcendentals=0),
    )


def in_hbm(shard):
    return pltpu.with_memory_space_constraint(shard[0, 0], pltpu.HBM)


def from_behind(value, down, right):
    rows, columns = lax.axis_size("row"), lax.axis_size("col")
    pairs = [
        (i * columns + j, (i + down) % rows * columns + (j + right) % columns)
        for i in range(rows)
        for j in range(columns)
    ]
    return lax.ppermute(value, ("row", "col"), pairs)


def step(corner, top_edge, left_edge, site_tensor, sketch, grad_left, grad_top):
    site = site_tensor.reshape(2, DD, DD)
    left_used = from_behind(left_edge[0, 0], 0, 1)
    top_used = from_behind(top_edge[0, 0], 1, 0)
    corner_used = from_behind(corner[0, 0], 1, 1)
    rows = pltpu.VMEM((CHI * LEAP, WIDE), F32)
    edge = pltpu.VMEM((CHI, ORDER), BF)
    here = pl.BlockSpec(memory_space=pltpu.HBM)
    a_mat, ket, bra, cols, turned, gwide = call(
        prepare_kernel,
        (
            shape(256, 256), shape(2, 256, 256), shape(2, 256, 256), shape(512, 256), shape(256, 512), shape(128, 2048),
        ),
        [rows, edge, edge, edge, pltpu.SemaphoreType.DMA((3,))],
        10**7, 2 * 10**6,
        [pl.BlockSpec(memory_space=pltpu.VMEM), here, here, here],
        room=PREP,
    )(site, in_hbm(sketch), in_hbm(grad_top), in_hbm(grad_left))
    sketched, rightward, tops, first, lwide, second, quad = call(
        forward_kernel,
        (
            shape(CHI, ORDER), shape(CHI, ORDER),
            shape(512, WIDE), shape(512, WIDE), shape(WIDE, 2048), shape(256, 4096), shape(512, 2048),
        ),
        [rows],
        2 * 10**9, 4 * 10**6,
    )(corner_used, top_used, left_used, a_mat, turned)
    sketch_beside = from_behind(sketched, 0, -1)
    sketch_below = from_behind(sketched, -1, 0)
    from_left = from_behind(rightward, 0, 1)
    downward = call(downward_kernel, shape(CHI, ORDER), [rows], 3 * 10**8, 3 * 10**6)(quad, gwide)
    from_above = from_behind(downward, 1, 0)
    part = call(
        partial_kernel, shape(512, 2048, dtype=F32),
        [rows, pltpu.VMEM((512, 256), BF), pltpu.VMEM((256, 2048), BF)],
        5 * 10**8, 5 * 10**6,
    )(sketch_below, sketch_beside, cols, gwide)
    grad_lefted, dquad, dsecond = call(
        backward_kernel,
        (shape(CHI, ORDER), shape(256, 4096), shape(512, 2048)),
        [pltpu.VMEM((128, 2048), BF)],
        2 * 10**9, 8 * 10**6,
    )(from_above, from_left, part, cols, a_mat, first)
    left_result = from_behind(grad_lefted, 0, -1)
    grad_topped, grad_cornered = call(
        edges_kernel, (shape(CHI, ORDER), shape(CHI, CHI)), [rows], 3 * 10**8, 3 * 10**6
    )(dsecond, lwide, tops, corner_used)
    top_result = from_behind(grad_topped, -1, 0)
    corner_result = from_behind(grad_cornered, -1, -1)
    site_result = call(site_kernel, shape(2, DD, DD, dtype=F32), [], 10**9, 5 * 10**6)(dquad, second, ket, bra)
    corner_result, top_result, left_result = call(
        finish_kernel,
        (shape(CHI, CHI), shape(CHI, ORDER), shape(CHI, ORDER)),
        [pltpu.SemaphoreType.DMA((3,))],
        0, 6 * 10**5,
        [pl.BlockSpec(memory_space=pltpu.VMEM)] * 3,
        (here, here, here),
    )(corner_result, top_result, left_result)
    return (
        corner_result[None, None],
        top_result[None, None],
        left_result[None, None],
        site_result.reshape(site_tensor.shape),
    )


def solution(mesh):
    flat = P("row", "col", None, None)
    deep = P("row", "col", None, None, None, None, None)
    return jax.shard_map(
        step,
        mesh=mesh,
        in_specs=(flat, flat, flat, deep, flat, flat, flat),
        out_specs=(flat, flat, flat, deep),
        check_vma=False,
    )
```

```python
import jax
import jax.numpy as jnp
from jax import lax
from jax.experimental import pallas as pl
from jax.experimental.pallas import tpu as pltpu
from jax.sharding import PartitionSpec as P


BF = jnp.bfloat16
F32 = jnp.float32
CHI = 64
DD = 16
ORDER = DD * CHI
HALF = CHI // 2
WIDE = 2 * CHI
LEAP = DD + 1
PREP = 20 << 20


def dot(lhs, rhs):
    return jnp.dot(lhs, rhs, preferred_element_type=F32)


def dot_nt(lhs, rhs):
    return lax.dot_general(lhs, rhs, (((1,), (1,)), ((), ())), preferred_element_type=F32)


def dot_tn(lhs, rhs):
    return lax.dot_general(lhs, rhs, (((0,), (0,)), ((), ())), preferred_element_type=F32)


def iota(shape, axis):
    return lax.broadcasted_iota(jnp.int32, shape, axis)


def first_half(shape):
    return iota(shape, 1) % WIDE < CHI


def to_rows(nat, rows_ref, out_ref, column):
    turned = jnp.concatenate([nat, nat], axis=0).T.astype(F32)
    for leg in range(DD):
        rows_ref[pl.ds(leg, CHI, stride=LEAP), :] = turned[leg * CHI : (leg + 1) * CHI]
    low = first_half((DD, WIDE))
    for at in range(HALF):
        even = rows_ref[2 * at * LEAP : 2 * at * LEAP + DD, :]
        odd = rows_ref[(2 * at + 1) * LEAP : (2 * at + 1) * LEAP + DD, :]
        out_ref[at * DD : (at + 1) * DD, column : column + WIDE] = jnp.where(low, even, odd).astype(BF)


def from_rows(value, rows_ref):
    for at in range(HALF):
        tile = value[at * DD : (at + 1) * DD, :]
        rows_ref[2 * at * LEAP : 2 * at * LEAP + DD, :] = tile
        rows_ref[(2 * at + 1) * LEAP : (2 * at + 1) * LEAP + DD, :] = tile
    legs = [rows_ref[pl.ds(leg, CHI, stride=LEAP), :].astype(BF) for leg in range(DD)]
    turned = jnp.concatenate(legs, axis=0).T
    even = iota((CHI, ORDER), 1) % 2 == 0
    return jnp.where(even, turned[:CHI], turned[CHI:])


def spread(nat, out_ref, row):
    value = nat.astype(F32)
    low = first_half((CHI, WIDE))
    zero = jnp.zeros((CHI, WIDE), F32)
    for pair in range(DD // 2):
        tile = value[:, pair * WIDE : (pair + 1) * WIDE]
        swapped = pltpu.roll(tile, CHI, 1)
        at = 2 * pair * WIDE
        out_ref[row : row + CHI, at : at + WIDE] = jnp.where(low, tile, zero).astype(BF)
        out_ref[row + CHI : row + WIDE, at : at + WIDE] = jnp.where(low, zero, swapped).astype(BF)
        at = at + WIDE
        out_ref[row : row + CHI, at : at + WIDE] = jnp.where(low, swapped, zero).astype(BF)
        out_ref[row + CHI : row + WIDE, at : at + WIDE] = jnp.where(low, zero, tile).astype(BF)


def gather_pair(value):
    low = first_half((CHI, WIDE))
    even, odd = value[:CHI], value[CHI:]
    stay = jnp.where(low, even[:, :WIDE], odd[:, WIDE:])
    move = jnp.where(low, even[:, WIDE:], odd[:, :WIDE])
    return stay + pltpu.roll(move, CHI, 1)


def leg_maps():
    column = iota((DD, 2 * WIDE), 1)
    small = iota((DD, 2 * WIDE), 0)
    ket_c = ((column // 4) % 4) * 4 + column // 64 == small
    bra_c = (column % 4) * 4 + (column // 16) % 4 == small
    return ket_c.astype(BF), bra_c.astype(BF)


def prepare_kernel(
    site_ref, sketch_hbm, gtop_hbm, gleft_hbm,
    a_ref, ket_ref, bra_ref, cols_ref, turned_ref, gwide_ref,
    rows_ref, sketch_ref, gtop_ref, gleft_ref, sems,
):
    copies = [
        pltpu.make_async_copy(source, target, sems.at[at])
        for at, (source, target) in enumerate(
            ((gtop_hbm, gtop_ref), (sketch_hbm, sketch_ref), (gleft_hbm, gleft_ref))
        )
    ]
    for copy in copies:
        copy.start()
    ket_map, bra_map = leg_maps()
    total = None
    for phys in range(2):
        site = site_ref[phys]
        ket = dot_tn(ket_map, dot_tn(site, ket_map).astype(BF))
        bra = dot_tn(bra_map, dot_tn(site, bra_map).astype(BF))
        ket_ref[phys] = ket.astype(BF)
        bra_ref[phys] = bra.astype(BF)
        total = ket * bra if total is None else total + ket * bra
    a_ref[...] = total.astype(BF)
    copies[0].wait()
    to_rows(gtop_ref[...], rows_ref, cols_ref, 0)
    copies[1].wait()
    to_rows(sketch_ref[...], rows_ref, cols_ref, WIDE)
    turned_ref[...] = cols_ref[...].T
    copies[2].wait()
    spread(gleft_ref[...], gwide_ref, 0)


def corner_pair(corner):
    nothing = jnp.zeros((CHI, CHI), BF)
    return jnp.concatenate(
        [jnp.concatenate([corner, nothing], axis=1), jnp.concatenate([nothing, corner], axis=1)], axis=0
    )


def turn_kernel(in_ref, out_ref, rows_ref):
    to_rows(in_ref[...], rows_ref, out_ref, 0)


def forward_kernel(
    corner_ref, tops_ref, left_ref, a_ref, turned_ref,
    sketched_ref, rightward_ref, first_ref, lwide_ref, second_ref, quad_ref,
):
    first_ref[...] = dot_nt(tops_ref[...], corner_pair(corner_ref[...])).astype(BF)
    spread(left_ref[...], lwide_ref, 0)

    def second_step(pair, carry):
        at = pl.multiple_of(pair * 2 * WIDE, 2 * WIDE)
        block = dot(first_ref[...], lwide_ref[:, pl.ds(at, 2 * WIDE)]).astype(BF)
        row = pl.multiple_of(pair * 2 * DD, 2 * DD)
        for one in range(HALF):
            piece = block[one * DD : (one + 1) * DD]
            second_ref[pl.ds(row, DD), one * WIDE : (one + 1) * WIDE] = piece[:, :WIDE]
            second_ref[pl.ds(row + DD, DD), one * WIDE : (one + 1) * WIDE] = piece[:, WIDE:]
        return carry

    lax.fori_loop(0, DD // 2, second_step, 0, unroll=8)

    def quad_step(pair, carry):
        at = pl.multiple_of(pair * 2 * WIDE, 2 * WIDE)
        block = dot(a_ref[...], second_ref[:, pl.ds(at, 2 * WIDE)]).astype(BF)
        row = pl.multiple_of(pair * 2 * DD, 2 * DD)
        for leg in range(DD):
            piece = block[leg * DD : (leg + 1) * DD]
            quad_ref[pl.ds(row, DD), leg * WIDE : (leg + 1) * WIDE] = piece[:, :WIDE]
            quad_ref[pl.ds(row + DD, DD), leg * WIDE : (leg + 1) * WIDE] = piece[:, WIDE:]
        return carry

    lax.fori_loop(0, HALF // 2, quad_step, 0, unroll=16)

    for pair in range(DD // 2):
        at = pair * 2 * WIDE
        block = dot(turned_ref[...], quad_ref[:, at : at + 2 * WIDE])
        rightward_ref[:, pair * WIDE : (pair + 1) * WIDE] = gather_pair(block[:WIDE]).astype(BF)
        sketched_ref[:, pair * WIDE : (pair + 1) * WIDE] = gather_pair(block[WIDE:]).astype(BF)


def downward_kernel(quad_ref, gwide_ref, downward_ref, rows_ref):
    down = dot_nt(quad_ref[...], gwide_ref[...])
    downward_ref[...] = from_rows(down, rows_ref)


def partial_kernel(below_ref, beside_ref, cols_ref, gwide_ref, part_ref, rows_ref, right_ref, left_ref):
    to_rows(below_ref[...], rows_ref, right_ref, 0)
    right_ref[:, WIDE:] = cols_ref[:, :WIDE]
    left_ref[:WIDE, :] = gwide_ref[...]
    spread(beside_ref[...], left_ref, WIDE)

    def step(pair, carry):
        at = pl.multiple_of(pair * 2 * WIDE, 2 * WIDE)
        part_ref[:, pl.ds(at, 2 * WIDE)] = dot(right_ref[...], left_ref[:, pl.ds(at, 2 * WIDE)])
        return carry

    lax.fori_loop(0, DD // 2, step, 0, unroll=8)


def backward_kernel(
    above_ref, behind_ref, part_ref, cols_ref, a_ref, first_ref,
    left_out_ref, dquad_ref, dsecond_ref,
    left_ref,
):
    arrived = (above_ref[...].astype(F32) + behind_ref[...].astype(F32)).astype(BF)
    spread(arrived, left_ref, 0)

    def dquad_step(pair, carry):
        at = pl.multiple_of(pair * 2 * WIDE, 2 * WIDE)
        block = dot(cols_ref[:, WIDE:], left_ref[:, pl.ds(at, 2 * WIDE)])
        block = (block + part_ref[:, pl.ds(at, 2 * WIDE)]).astype(BF)
        row = pl.multiple_of(pair * 2 * DD, 2 * DD)
        for one in range(HALF):
            piece = block[one * DD : (one + 1) * DD]
            dquad_ref[pl.ds(row, DD), one * WIDE : (one + 1) * WIDE] = piece[:, :WIDE]
            dquad_ref[pl.ds(row + DD, DD), one * WIDE : (one + 1) * WIDE] = piece[:, WIDE:]
        return carry

    lax.fori_loop(0, DD // 2, dquad_step, 0, unroll=8)
    a_turned = a_ref[...].T

    def dsecond_step(pair, carry):
        at = pl.multiple_of(pair * 2 * WIDE, 2 * WIDE)
        block = dot(a_turned, dquad_ref[:, pl.ds(at, 2 * WIDE)]).astype(BF)
        row = pl.multiple_of(pair * 2 * DD, 2 * DD)
        for leg in range(DD):
            piece = block[leg * DD : (leg + 1) * DD]
            dsecond_ref[pl.ds(row, DD), leg * WIDE : (leg + 1) * WIDE] = piece[:, :WIDE]
            dsecond_ref[pl.ds(row + DD, DD), leg * WIDE : (leg + 1) * WIDE] = piece[:, WIDE:]
        return carry

    lax.fori_loop(0, HALF // 2, dsecond_step, 0, unroll=16)

    first_turned = first_ref[...].T
    for pair in range(DD // 2):
        at = pair * 2 * WIDE
        block = dot(first_turned, dsecond_ref[:, at : at + 2 * WIDE])
        left_out_ref[:, pair * WIDE : (pair + 1) * WIDE] = gather_pair(block).astype(BF)


def edges_kernel(dsecond_ref, lwide_ref, tops_ref, corner_ref, top_out_ref, corner_out_ref, rows_ref):
    dfirst = dot_nt(dsecond_ref[...], lwide_ref[...]).astype(BF)
    dtop = dot(dfirst, corner_pair(corner_ref[...]))
    top_out_ref[...] = from_rows(dtop, rows_ref)
    dcorner = dot_tn(dfirst, tops_ref[...])
    corner_out_ref[...] = (dcorner[:CHI, :CHI] + pltpu.roll(dcorner[CHI:], CHI, 1)[:, :CHI]).astype(BF)


def site_kernel(dquad_ref, second_ref, ket_ref, bra_ref, out_ref):
    grad = dot_nt(dquad_ref[...], second_ref[...])
    ket_map, bra_map = leg_maps()
    total = None
    for other_ref, leg_map in ((ket_ref, bra_map), (bra_ref, ket_map)):
        pieces = [(grad * other_ref[phys].astype(F32)).astype(BF) for phys in range(2)]
        half = dot_nt(jnp.concatenate(pieces, axis=0), leg_map).astype(BF)
        term = dot(leg_map, jnp.concatenate([half[: 2 * WIDE], half[2 * WIDE :]], axis=1))
        total = term if total is None else total + term
    turned = total.T
    out_ref[0] = turned[:DD]
    out_ref[1] = turned[DD:]


def finish_kernel(*refs):
    count = len(refs) // 2
    sems = refs[-1]
    copies = [pltpu.make_async_copy(refs[at], refs[count + at], sems.at[at]) for at in range(count)]
    for copy in copies:
        copy.start()
    for copy in copies:
        copy.wait()


def shape(*dims, dtype=BF):
    return jax.ShapeDtypeStruct(dims, dtype)


def call(kernel, outs, scratch, flops, moved, specs=None, out_specs=None, room=20 << 20):
    extra = {} if specs is None else {"in_specs": specs}
    if out_specs is not None:
        extra["out_specs"] = out_specs
    return pl.pallas_call(
        kernel,
        out_shape=outs,
        **extra,
        scratch_shapes=scratch,
        compiler_params=pltpu.CompilerParams(vmem_limit_bytes=room),
        cost_estimate=pl.CostEstimate(flops=flops, bytes_accessed=moved, transcendentals=0),
    )


def in_hbm(shard):
    return pltpu.with_memory_space_constraint(shard[0, 0], pltpu.HBM)


def from_behind(value, down, right):
    rows, columns = lax.axis_size("row"), lax.axis_size("col")
    pairs = [
        (i * columns + j, (i + down) % rows * columns + (j + right) % columns)
        for i in range(rows)
        for j in range(columns)
    ]
    return lax.ppermute(value, ("row", "col"), pairs)


def step(corner, top_edge, left_edge, site_tensor, sketch, grad_left, grad_top):
    site = site_tensor.reshape(2, DD, DD)
    left_used = from_behind(left_edge[0, 0], 0, 1)
    top_used = from_behind(top_edge[0, 0], 1, 0)
    corner_used = from_behind(corner[0, 0], 1, 1)
    rows = pltpu.VMEM((CHI * LEAP, WIDE), F32)
    edge = pltpu.VMEM((CHI, ORDER), BF)
    here = pl.BlockSpec(memory_space=pltpu.HBM)
    a_mat, ket, bra, cols, turned, gwide = call(
        prepare_kernel,
        (
            shape(256, 256), shape(2, 256, 256), shape(2, 256, 256), shape(512, 256), shape(256, 512), shape(128, 2048),
        ),
        [rows, edge, edge, edge, pltpu.SemaphoreType.DMA((3,))],
        10**7, 2 * 10**6,
        [pl.BlockSpec(memory_space=pltpu.VMEM), here, here, here],
        room=PREP,
    )(site, in_hbm(sketch), in_hbm(grad_top), in_hbm(grad_left))
    tops = call(turn_kernel, shape(512, WIDE), [rows], 10**6, 5 * 10**5)(top_used)
    sketched, rightward, first, lwide, second, quad = call(
        forward_kernel,
        (
            shape(CHI, ORDER), shape(CHI, ORDER),
            shape(512, WIDE), shape(WIDE, 2048), shape(256, 4096), shape(512, 2048),
        ),
        [],
        2 * 10**9, 4 * 10**6,
    )(corner_used, tops, left_used, a_mat, turned)
    sketch_beside = from_behind(sketched, 0, -1)
    sketch_below = from_behind(sketched, -1, 0)
    from_left = from_behind(rightward, 0, 1)
    downward = call(downward_kernel, shape(CHI, ORDER), [rows], 3 * 10**8, 3 * 10**6)(quad, gwide)
    from_above = from_behind(downward, 1, 0)
    part = call(
        partial_kernel, shape(512, 2048, dtype=F32),
        [rows, pltpu.VMEM((512, 256), BF), pltpu.VMEM((256, 2048), BF)],
        5 * 10**8, 5 * 10**6,
    )(sketch_below, sketch_beside, cols, gwide)
    grad_lefted, dquad, dsecond = call(
        backward_kernel,
        (shape(CHI, ORDER), shape(256, 4096), shape(512, 2048)),
        [pltpu.VMEM((128, 2048), BF)],
        2 * 10**9, 8 * 10**6,
    )(from_above, from_left, part, cols, a_mat, first)
    left_result = from_behind(grad_lefted, 0, -1)
    grad_topped, grad_cornered = call(
        edges_kernel, (shape(CHI, ORDER), shape(CHI, CHI)), [rows], 3 * 10**8, 3 * 10**6
    )(dsecond, lwide, tops, corner_used)
    top_result = from_behind(grad_topped, -1, 0)
    corner_result = from_behind(grad_cornered, -1, -1)
    site_result = call(site_kernel, shape(2, DD, DD, dtype=F32), [], 10**9, 5 * 10**6)(dquad, second, ket, bra)
    whole = pl.BlockSpec(memory_space=pltpu.VMEM)
    (left_result,) = call(
        finish_kernel, (shape(CHI, ORDER),), [pltpu.SemaphoreType.DMA((1,))], 0, 3 * 10**5, [whole], (here,)
    )(left_result)
    corner_result, top_result = call(
        finish_kernel,
        (shape(CHI, CHI), shape(CHI, ORDER)),
        [pltpu.SemaphoreType.DMA((2,))],
        0, 3 * 10**5,
        [whole] * 2,
        (here, here),
    )(corner_result, top_result)
    return (
        corner_result[None, None],
        top_result[None, None],
        left_result[None, None],
        site_result.reshape(site_tensor.shape),
    )


def solution(mesh):
    flat = P("row", "col", None, None)
    deep = P("row", "col", None, None, None, None, None)
    return jax.shard_map(
        step,
        mesh=mesh,
        in_specs=(flat, flat, flat, deep, flat, flat, flat),
        out_specs=(flat, flat, flat, deep),
        check_vma=False,
    )
```
